32 devices in a mesh: groups: 2 (over y), tensor: 16 (over z, x, core).
Axes of the slice: x: 2, y: 2, z: 4, core: 2. Of those that a mesh axis runs over, the one named last changes fastest.
Arguments:
- tokens: bfloat16 [64, 8192], P(('groups', 'tensor')), parts along dimension 0, may hold values from -6 to 6
- gate_weight: bfloat16 [8192, 28672], P(None, 'tensor'), may hold values from -0.0625 to 0.0625
- up_weight: bfloat16 [8192, 28672], P(None, 'tensor'), may hold values from -0.0625 to 0.0625
- local_factor: bfloat16 [1792, 1792], replicated, may hold values from -0.125 to 0.125
- row_scale: float32 [64], P('groups'), parts along dimension 0, may hold values from 0.25 to 4
- down_weight: bfloat16 [28672, 8192], P('tensor'), may hold values from -0.03125 to 0.03125
Outputs:
- output: bfloat16 [64, 8192], P(('groups', 'tensor')), parts along dimension 0
The draws below stay inside these ranges and needn't reach their ends.
There are 2 independent parts, one for each index of `groups`. The reference program is written for one: setup_inputs(seed, part) draws one part's arguments, and reference() takes and returns one part's arrays. A program takes and returns all parts, laid end to end along the dimension named above; an argument that names none is the same for every part. Nothing has to cross between parts.
All inputs are finite; a program needn't handle non-finite values.
Results may differ from the reference program's by a relative error of at most 0.0061.
Values may be sent and summed in bfloat16 or wider, within the bound.
A program may use at most 128 MiB of HBM per device.

```python
import math
import jax
import jax.numpy as jnp
from jax import lax

D = 8192
FF = 28672
ROWS = 32
LOC = 1792
N_TENSOR = 16


def shard_levels(key, extent, cuts, low, largest):
    level = 1.0
    for position, blocks in cuts:
        draws = jax.random.uniform(jax.random.fold_in(jax.random.fold_in(key, 6), position), (blocks,), jnp.float32, low / len(cuts), largest / len(cuts))
        level = level * jnp.repeat(jnp.exp(draws), extent[position] // blocks).reshape((-1,) + (1,) * (len(extent) - 1 - position))
    return level


def noise(stream_key, dims, deviation, limit, cuts=(), kind=jnp.bfloat16):
    array = deviation * jax.random.normal(stream_key, dims, jnp.float32)
    if cuts:
        array = array * shard_levels(stream_key, dims, cuts, -0.22, 0.18)
    return jnp.clip(array, -limit, limit).astype(kind)


def setup_inputs(seed: int = 0, part: int = 0) -> dict:
    key_of = jax.random.split(jax.random.key(seed), 7)
    part_keys = jax.random.split(jax.random.fold_in(key_of[6], part), 7)
    return {
        "tokens": noise(part_keys[0], (ROWS, D), 1.0, 6.0, ((0, 16),)),
        "gate_weight": noise(key_of[1], (D, FF), D ** -0.5, 0.0625, ((1, 16),)),
        "up_weight": noise(key_of[2], (D, FF), D ** -0.5, 0.0625, ((1, 16),)),
        "local_factor": noise(key_of[3], (LOC, LOC), LOC ** -0.5, 0.125),
        "row_scale": jnp.clip(jnp.exp(jax.random.uniform(part_keys[4], (ROWS,), jnp.float32, math.log(0.25), math.log(4.0))), 0.25, 4.0),
        "down_weight": noise(key_of[5], (FF, D), FF ** -0.5, 0.03125, ((0, 16),)),
    }


def hadamard(count):
    first = jnp.arange(count, dtype=jnp.int32)[:, None]
    second = jnp.arange(count, dtype=jnp.int32)[None, :]
    both = jnp.bitwise_and(first, second)
    parity = jnp.zeros((count, count), jnp.int32)
    for shift_bit in range(max(count.bit_length() - 1, 0)):
        parity = parity + jnp.bitwise_and(jnp.right_shift(both, shift_bit), 1)
    return (1 - 2 * jnp.bitwise_and(parity, 1)).astype(jnp.float32)

def reference(tokens, gate_weight, up_weight, local_factor, row_scale, down_weight):
    gate = jnp.dot(tokens, gate_weight, preferred_element_type=jnp.float32)
    up_part = jnp.dot(tokens, up_weight, preferred_element_type=jnp.float32)
    hidden = (jax.nn.silu(gate) * up_part).astype(jnp.bfloat16)
    blocks = hidden.reshape(ROWS, N_TENSOR, LOC)
    local = jnp.einsum('rsi,ij->rsj', blocks.astype(jnp.float32), local_factor.astype(jnp.float32))
    matrix = hadamard(N_TENSOR)
    mixed = jnp.einsum('ts,rsj->rtj', matrix, local, precision=lax.Precision.HIGHEST) / jnp.sqrt(jnp.float32(N_TENSOR))
    mixed = mixed.reshape(ROWS, FF)
    clipped = (1.5 * jnp.tanh(mixed / (1.5 * row_scale[:, None]))).astype(jnp.bfloat16)
    return jnp.dot(clipped, down_weight, preferred_element_type=jnp.float32).astype(jnp.bfloat16)
```

```python
import functools
import jax
import jax.numpy as jnp
from jax import lax
from jax.experimental import pallas as pl
from jax.experimental.pallas import tpu as pltpu
from jax.sharding import PartitionSpec as P

CORES = 2
SIDE = 2
SLOTS = 6
K_STEPS = 16
GATHER_STEPS = 4
DOWN_STEPS = 8
LAGS = (2, 5, 10)


def swapped(block, axis, distance):
    count = lax.axis_size(axis)
    route = []
    for low in range(count):
        high = low | 1 << distance
        if high != low and high < count:
            route += [(low, high), (high, low)]
    return lax.ppermute(block, axis, route)


def plain_body(tokens, gate_weight, up_weight, local_factor, row_scale, down_weight):
    count = lax.axis_size("tensor")
    own = lax.axis_index("tensor")
    piece = lax.all_gather(tokens, "tensor", axis=0, tiled=True)
    gate = jnp.dot(piece, gate_weight, preferred_element_type=jnp.float32)
    up_part = jnp.dot(piece, up_weight, preferred_element_type=jnp.float32)
    hidden = (jax.nn.silu(gate) * up_part).astype(jnp.bfloat16)
    local = jnp.dot(hidden, local_factor, preferred_element_type=jnp.float32)
    norm = 1.0 / jnp.sqrt(jnp.float32(count))
    mixed = local
    for level in range(count.bit_length() - 1):
        other = swapped(mixed, "tensor", level)
        upper = jnp.bitwise_and(jnp.right_shift(own, level), 1) == 1
        mixed = jnp.where(upper, other - mixed, mixed + other)
    mixed = mixed * norm
    clipped = (1.5 * jnp.tanh(mixed / (1.5 * row_scale[:, None]))).astype(jnp.bfloat16)
    summed = jnp.dot(clipped, down_weight, preferred_element_type=jnp.float32)
    for level in reversed(range(count.bit_length() - 1)):
        half = summed.shape[0] // 2
        lower = summed[:half]
        higher = summed[half:]
        upper = jnp.bitwise_and(jnp.right_shift(own, level), 1) == 1
        keep = jnp.where(upper, higher, lower)
        send = jnp.where(upper, lower, higher)
        summed = keep + swapped(send, "tensor", level)
    return summed.astype(jnp.bfloat16)


def remote(src, dst, send_sem, recv_sem, target):
    return pltpu.make_async_remote_copy(
        src_ref=src, dst_ref=dst, send_sem=send_sem, recv_sem=recv_sem,
        device_id={"tensor": target}, device_id_type=pl.DeviceIdType.MESH)


def kernel(n, tok, gate, up, loc, scale, down, out,
           gbuf, ubuf, lbuf, dbuf, xbuf, x32, xb, acc_g, acc_u, hbuf,
           sbuf, rbuf, c2, cbuf, c32, cb,
           keep1, send1, rec1, keep2, send2, rec2, zkeep, zsend, zrec,
           gsem, usem, lsem, dsem, own_sem,
           s1s, s1r, s2s, s2r, s3s, s3r, m1s, m1r, m2s, m2r,
           r1s, r1r, r2s, r2r, r3s, r3r):
    rows, width = tok.shape
    hid = gate.shape[1]
    zs = n // (SIDE * CORES)
    kc = width // K_STEPS
    gc = width // GATHER_STEPS
    nc = width // DOWN_STEPS
    me = lax.axis_index("tensor")
    z = me // (SIDE * CORES)
    x = (me // CORES) % SIDE
    c = me % CORES

    def index(pz, px, pc):
        return (pz * SIDE + px) * CORES + pc

    def weights(k):
        slot = lax.rem(k, SLOTS)
        span = pl.ds(pl.multiple_of(k * kc, kc), kc)
        return (pltpu.make_async_copy(gate.at[span, :], gbuf.at[slot], gsem.at[slot]),
                pltpu.make_async_copy(up.at[span, :], ubuf.at[slot], usem.at[slot]))

    def down_copy(j):
        span = pl.ds(pl.multiple_of(j * nc, nc), nc)
        return pltpu.make_async_copy(down.at[:, span], dbuf.at[j], dsem.at[j])

    own_block = pltpu.make_async_copy(tok, xbuf.at[z, x, c], own_sem.at[0])
    own_block.start()
    for k in range(SLOTS):
        for copy in weights(k):
            copy.start()
    local_copy = pltpu.make_async_copy(loc, lbuf, lsem)
    local_copy.start()
    down_copy(0).start()

    barrier = pltpu.get_barrier_semaphore()

    @pl.loop(1, n)
    def _(d):
        pl.semaphore_signal(barrier, inc=1, device_id={"tensor": lax.rem(me + d, n)},
                            device_id_type=pl.DeviceIdType.MESH)
    pl.semaphore_wait(barrier, n - 1)

    def gather_z(a, d):
        cols = pl.ds(a * gc, gc)
        return remote(tok.at[:, cols], xbuf.at[z, x, c, :, cols], s1s.at[a, d - 1], s1r.at[a, d - 1],
                      index(lax.rem(z + d, zs), x, c))

    def gather_x(a):
        view = xbuf.at[:, x, c, :, pl.ds(a * gc, gc)]
        return remote(view, view, s2s.at[a], s2r.at[a], index(z, 1 - x, c))

    def gather_c(a):
        view = xbuf.at[:, :, c, :, pl.ds(a * gc, gc)]
        return remote(view, view, s3s.at[a], s3r.at[a], index(z, x, 1 - c))

    for a in range(GATHER_STEPS):
        for d in range(1, zs):
            gather_z(a, d).start()
    acc_g[...] = jnp.zeros_like(acc_g)
    acc_u[...] = jnp.zeros_like(acc_u)
    own_block.wait()
    per = K_STEPS // GATHER_STEPS
    places = [(pz, px, pc) for pc in range(CORES) for px in range(SIDE) for pz in range(zs)]

    def multiply(k, _):
        slot = lax.rem(k, SLOTS)
        for copy in weights(k):
            copy.wait()
        part = xb[k]
        acc_g[...] += jnp.dot(part, gbuf[slot], preferred_element_type=jnp.float32)
        acc_u[...] += jnp.dot(part, ubuf[slot], preferred_element_type=jnp.float32)

        @pl.when(k + SLOTS < K_STEPS)
        def _():
            for copy in weights(k + SLOTS):
                copy.start()

        @pl.when(k + SLOTS >= K_STEPS)
        def _():
            down_copy(k + SLOTS - K_STEPS + 1).start()
        return 0

    for i in range(GATHER_STEPS + 2):
        if i < GATHER_STEPS:
            for d in range(1, zs):
                gather_z(i, d).wait_recv()
            gather_x(i).start()
        if 1 <= i <= GATHER_STEPS:
            gather_x(i - 1).wait_recv()
            gather_c(i - 1).start()
        if i >= 2:
            a = i - 2
            gather_c(a).wait_recv()
            for p, place in enumerate(places):
                x32[p * rows:(p + 1) * rows, :] = xbuf[(*place, slice(None), pl.ds(a * gc, gc))].astype(jnp.float32)
            for b in range(per):
                xb[a * per + b] = x32[:, b * kc:(b + 1) * kc].astype(jnp.bfloat16)
            lax.fori_loop(a * per, (a + 1) * per, multiply, 0)
    for j in range(SLOTS + 1, DOWN_STEPS):
        down_copy(j).start()
    for a in range(GATHER_STEPS):
        for d in range(1, zs):
            gather_z(a, d).wait_send()
        gather_x(a).wait_send()
        gather_c(a).wait_send()

    hbuf[...] = (jax.nn.silu(acc_g[...]) * acc_u[...]).astype(jnp.bfloat16)
    local_copy.wait()
    acc_g[...] = jnp.dot(hbuf[...], lbuf[...], preferred_element_type=jnp.float32)
    for p, place in enumerate(places):
        sbuf[index(*place)] = acc_g[p * rows:(p + 1) * rows, :].astype(jnp.bfloat16)

    def exchange(src, dst, send_sem, recv_sem, copy_sem):
        def step(d):
            target = lax.rem(me + d, n)
            return remote(src.at[target], dst.at[me], send_sem.at[d - 1], recv_sem.at[d - 1], target)

        @pl.loop(1, n)
        def _(d):
            step(d).start()
        kept = pltpu.make_async_copy(src.at[me], dst.at[me], copy_sem)
        kept.start()
        kept.wait()

        @pl.loop(1, n)
        def _(d):
            step(d).wait()

    exchange(sbuf, rbuf, m1s, m1r, own_sem.at[1])

    block = 256 if hid % 256 == 0 else 128
    line = lax.broadcasted_iota(jnp.int32, (rows, block), 0)
    scales = jnp.zeros((rows, block), jnp.float32)
    for r in range(rows):
        scales = jnp.where(line == r, scale[me * rows + r], scales)
    inverse = 1.0 / (1.5 * scales)
    norm = 1.0 / (float(n) ** 0.5)

    @pl.loop(0, hid // block)
    def _(b):
        cols = pl.ds(pl.multiple_of(b * block, block), block)
        parts = [rbuf[s, :, cols].astype(jnp.float32) for s in range(n)]
        for level in range(n.bit_length() - 1):
            bit = 1 << level
            parts = [parts[t ^ bit] - parts[t] if t & bit else parts[t] + parts[t ^ bit] for t in range(n)]
        for t in range(n):
            c2[t, :, cols] = (1.5 * jnp.tanh((parts[t] * norm) * inverse)).astype(jnp.bfloat16)

    exchange(c2, cbuf, m2s, m2r, own_sem.at[2])
    for p, place in enumerate(places):
        c32[p * rows:(p + 1) * rows, :] = cbuf[index(*place)].astype(jnp.float32)
    cb[...] = c32[...].astype(jnp.bfloat16)

    half = n * rows // CORES
    quarter = half // SIDE

    def scatter_c(j):
        return remote(send1.at[j], rec1.at[j], r1s.at[j], r1r.at[j], index(z, x, 1 - c))

    def scatter_x(j):
        return remote(send2.at[j], rec2.at[j], r2s.at[j], r2r.at[j], index(z, 1 - x, c))

    def scatter_z(j, d):
        pz = lax.rem(z + d, zs)
        return remote(zsend.at[j, pz], zrec.at[j, d - 1], r3s.at[j, d - 1], r3r.at[j, d - 1], index(pz, x, c))

    for i in range(DOWN_STEPS + LAGS[2]):
        if i < DOWN_STEPS:
            j = i
            down_copy(j).wait()
            part = jnp.dot(cb[...], dbuf[j], preferred_element_type=jnp.float32)
            keep1[j] = jnp.where(c == 1, part[half:], part[:half])
            send1[j] = jnp.where(c == 1, part[:half], part[half:]).astype(jnp.bfloat16)
            scatter_c(j).start()
        j = i - LAGS[0]
        if 0 <= j < DOWN_STEPS:
            scatter_c(j).wait()
            part = keep1[j] + rec1[j].astype(jnp.float32)
            keep2[j] = jnp.where(x == 1, part[quarter:], part[:quarter])
            send2[j] = jnp.where(x == 1, part[:quarter], part[quarter:]).astype(jnp.bfloat16)
            scatter_x(j).start()
        j = i - LAGS[1]
        if 0 <= j < DOWN_STEPS:
            scatter_x(j).wait()
            keep2[j] = keep2[j] + rec2[j].astype(jnp.float32)
            for pz in range(zs):
                piece = keep2[j, pz * rows:(pz + 1) * rows, :]
                zkeep[j, pz] = piece
                zsend[j, pz] = piece.astype(jnp.bfloat16)
            for d in range(1, zs):
                scatter_z(j, d).start()
        j = i - LAGS[2]
        if 0 <= j < DOWN_STEPS:
            total = zkeep[j, z]
            for d in range(1, zs):
                scatter_z(j, d).wait()
                total = total + zrec[j, d - 1].astype(jnp.float32)
            out[:, j * nc:(j + 1) * nc] = total.astype(jnp.bfloat16)


def kernel_body(tokens, gate_weight, up_weight, local_factor, row_scale, down_weight):
    n = lax.axis_size("tensor")
    rows, width = tokens.shape
    hid = gate_weight.shape[1]
    zs = n // (SIDE * CORES)
    kc = width // K_STEPS
    gc = width // GATHER_STEPS
    nc = width // DOWN_STEPS
    half = n * rows // CORES
    quarter = half // SIDE
    bf16, f32 = jnp.bfloat16, jnp.float32
    dma = pltpu.SemaphoreType.DMA
    vmem = pl.BlockSpec(memory_space=pltpu.VMEM)
    hbm = pl.BlockSpec(memory_space=pl.ANY)
    return pl.pallas_call(
        functools.partial(kernel, n),
        out_shape=jax.ShapeDtypeStruct((rows, width), bf16),
        in_specs=[vmem, hbm, hbm, hbm, pl.BlockSpec(memory_space=pltpu.SMEM), hbm],
        out_specs=vmem,
        scratch_shapes=[
            pltpu.VMEM((SLOTS, kc, hid), bf16),
            pltpu.VMEM((SLOTS, kc, hid), bf16),
            pltpu.VMEM((hid, hid), bf16),
            pltpu.VMEM((DOWN_STEPS, hid, nc), bf16),
            pltpu.VMEM((zs, SIDE, CORES, rows, width), bf16),
            pltpu.VMEM((n * rows, gc), f32),
            pltpu.VMEM((K_STEPS, n * rows, kc), bf16),
            pltpu.VMEM((n * rows, hid), f32),
            pltpu.VMEM((n * rows, hid), f32),
            pltpu.VMEM((n * rows, hid), bf16),
            pltpu.VMEM((n, rows, hid), bf16),
            pltpu.VMEM((n, rows, hid), bf16),
            pltpu.VMEM((n, rows, hid), bf16),
            pltpu.VMEM((n, rows, hid), bf16),
            pltpu.VMEM((n * rows, hid), f32),
            pltpu.VMEM((n * rows, hid), bf16),
            pltpu.VMEM((DOWN_STEPS, half, nc), f32),
            pltpu.VMEM((DOWN_STEPS, half, nc), bf16),
            pltpu.VMEM((DOWN_STEPS, half, nc), bf16),
            pltpu.VMEM((DOWN_STEPS, quarter, nc), f32),
            pltpu.VMEM((DOWN_STEPS, quarter, nc), bf16),
            pltpu.VMEM((DOWN_STEPS, quarter, nc), bf16),
            pltpu.VMEM((DOWN_STEPS, zs, rows, nc), f32),
            pltpu.VMEM((DOWN_STEPS, zs, rows, nc), bf16),
            pltpu.VMEM((DOWN_STEPS, zs - 1, rows, nc), bf16),
            dma((SLOTS,)), dma((SLOTS,)), dma, dma((DOWN_STEPS,)), dma((3,)),
            dma((GATHER_STEPS, zs - 1)), dma((GATHER_STEPS, zs - 1)),
            dma((GATHER_STEPS,)), dma((GATHER_STEPS,)),
            dma((GATHER_STEPS,)), dma((GATHER_STEPS,)),
            dma((n - 1,)), dma((n - 1,)), dma((n - 1,)), dma((n - 1,)),
            dma((DOWN_STEPS,)), dma((DOWN_STEPS,)),
            dma((DOWN_STEPS,)), dma((DOWN_STEPS,)),
            dma((DOWN_STEPS, zs - 1)), dma((DOWN_STEPS, zs - 1)),
        ],
        compiler_params=pltpu.CompilerParams(
            collective_id=0, has_side_effects=True, vmem_limit_bytes=67043328),
    )(tokens, gate_weight, up_weight, local_factor, row_scale, down_weight)


def body(tokens, gate_weight, up_weight, local_factor, row_scale, down_weight):
    n = lax.axis_size("tensor")
    rows, width = tokens.shape
    hid = gate_weight.shape[1]
    fits = (n == 1 << (n.bit_length() - 1) and n % (SIDE * CORES * 2) == 0 and hid % 128 == 0
            and width % (128 * K_STEPS) == 0 and n * rows <= 32)
    chosen = kernel_body if fits else plain_body
    return chosen(tokens, gate_weight, up_weight, local_factor, row_scale, down_weight)


def solution(mesh):
    in_specs = (
        P(("groups", "tensor"), None),
        P(None, "tensor"),
        P(None, "tensor"),
        P(),
        P("groups"),
        P("tensor", None),
    )
    out_specs = P(("groups", "tensor"), None)
    return jax.shard_map(body, mesh=mesh, in_specs=in_specs, out_specs=out_specs, check_vma=False)
```

```python
import functools
import jax
import jax.numpy as jnp
from jax import lax
from jax.experimental import pallas as pl
from jax.experimental.pallas import tpu as pltpu
from jax.sharding import PartitionSpec as P

CORES = 2
SIDE = 2
SLOTS = 6
K_STEPS = 16
GATHER_STEPS = 8
DOWN_STEPS = 8
LAGS = (3, 7, 12)
EARLY_DOWN = 2


def swapped(block, axis, distance):
    count = lax.axis_size(axis)
    route = []
    for low in range(count):
        high = low | 1 << distance
        if high != low and high < count:
            route += [(low, high), (high, low)]
    return lax.ppermute(block, axis, route)


def plain_body(tokens, gate_weight, up_weight, local_factor, row_scale, down_weight):
    count = lax.axis_size("tensor")
    own = lax.axis_index("tensor")
    piece = lax.all_gather(tokens, "tensor", axis=0, tiled=True)
    gate = jnp.dot(piece, gate_weight, preferred_element_type=jnp.float32)
    up_part = jnp.dot(piece, up_weight, preferred_element_type=jnp.float32)
    hidden = (jax.nn.silu(gate) * up_part).astype(jnp.bfloat16)
    local = jnp.dot(hidden, local_factor, preferred_element_type=jnp.float32)
    norm = 1.0 / jnp.sqrt(jnp.float32(count))
    mixed = local
    for level in range(count.bit_length() - 1):
        other = swapped(mixed, "tensor", level)
        upper = jnp.bitwise_and(jnp.right_shift(own, level), 1) == 1
        mixed = jnp.where(upper, other - mixed, mixed + other)
    mixed = mixed * norm
    clipped = (1.5 * jnp.tanh(mixed / (1.5 * row_scale[:, None]))).astype(jnp.bfloat16)
    summed = jnp.dot(clipped, down_weight, preferred_element_type=jnp.float32)
    for level in reversed(range(count.bit_length() - 1)):
        half = summed.shape[0] // 2
        lower = summed[:half]
        higher = summed[half:]
        upper = jnp.bitwise_and(jnp.right_shift(own, level), 1) == 1
        keep = jnp.where(upper, higher, lower)
        send = jnp.where(upper, lower, higher)
        summed = keep + swapped(send, "tensor", level)
    return summed.astype(jnp.bfloat16)


def remote(src, dst, send_sem, recv_sem, target):
    return pltpu.make_async_remote_copy(
        src_ref=src, dst_ref=dst, send_sem=send_sem, recv_sem=recv_sem,
        device_id={"tensor": target}, device_id_type=pl.DeviceIdType.MESH)


def kernel(n, tok, gate, up, loc, scale, down, out,
           gbuf, ubuf, lbuf, dbuf, xbuf, x32, xb, acc_g, acc_u, hbuf,
           sbuf, rbuf, c2, cbuf, c32, cb, pacc,
           keep1, send1, rec1, keep2, send2, rec2, zkeep, zsend, zrec,
           gsem, usem, lsem, dsem, own_sem,
           s1s, s1r, s3s, s3r, m1s, m1r, m2s, m2r,
           r1s, r1r, r2s, r2r, r3s, r3r):
    rows, width = tok.shape
    hid = gate.shape[1]
    zs = n // (SIDE * CORES)
    kc = width // K_STEPS
    gc = width // GATHER_STEPS
    nc = width // DOWN_STEPS
    me = lax.axis_index("tensor")
    z = me // (SIDE * CORES)
    x = (me // CORES) % SIDE
    c = me % CORES

    def index(pz, px, pc):
        return (pz * SIDE + px) * CORES + pc

    def weights(k):
        slot = lax.rem(k, SLOTS)
        span = pl.ds(pl.multiple_of(k * kc, kc), kc)
        return (pltpu.make_async_copy(gate.at[span, :], gbuf.at[slot], gsem.at[slot]),
                pltpu.make_async_copy(up.at[span, :], ubuf.at[slot], usem.at[slot]))

    def down_copy(j):
        span = pl.ds(pl.multiple_of(j * nc, nc), nc)
        return pltpu.make_async_copy(down.at[:, span], dbuf.at[j], dsem.at[j])

    own_block = pltpu.make_async_copy(tok, xbuf.at[me // CORES, c], own_sem)
    own_block.start()
    for k in range(SLOTS):
        for copy in weights(k):
            copy.start()
    local_copy = pltpu.make_async_copy(loc, lbuf, lsem)
    local_copy.start()
    for j in range(EARLY_DOWN):
        down_copy(j).start()

    barrier = pltpu.get_barrier_semaphore()

    @pl.loop(1, n)
    def _(d):
        pl.semaphore_signal(barrier, inc=1, device_id={"tensor": lax.rem(me + d, n)},
                            device_id_type=pl.DeviceIdType.MESH)
    pl.semaphore_wait(barrier, n - 1)

    chips = n // CORES
    chip = me // CORES

    def gather_chip(a, d):
        cols = pl.ds(a * gc, gc)
        target = lax.rem(chip + d, chips) * CORES + c
        return remote(tok.at[:, cols], xbuf.at[chip, c, :, cols], s1s.at[a, d - 1], s1r.at[a, d - 1], target)

    def gather_core(a):
        view = xbuf.at[:, c, :, pl.ds(a * gc, gc)]
        return remote(view, view, s3s.at[a], s3r.at[a], chip * CORES + 1 - c)

    for a in range(GATHER_STEPS):
        @pl.loop(1, chips)
        def _(d):
            gather_chip(a, d).start()
    acc_g[...] = jnp.zeros_like(acc_g)
    acc_u[...] = jnp.zeros_like(acc_u)
    own_block.wait()
    per = K_STEPS // GATHER_STEPS
    places = [(pz, px, pc) for pc in range(CORES) for px in range(SIDE) for pz in range(zs)]

    def multiply(k, _):
        slot = lax.rem(k, SLOTS)
        for copy in weights(k):
            copy.wait()
        part = xb[k]
        acc_g[...] += jnp.dot(part, gbuf[slot], preferred_element_type=jnp.float32)
        acc_u[...] += jnp.dot(part, ubuf[slot], preferred_element_type=jnp.float32)

        @pl.when(k + SLOTS < K_STEPS)
        def _():
            for copy in weights(k + SLOTS):
                copy.start()

        @pl.when(k + SLOTS >= K_STEPS)
        def _():
            down_copy(k + SLOTS - K_STEPS + EARLY_DOWN).start()
        return 0

    for i in range(GATHER_STEPS + 1):
        if i < GATHER_STEPS:
            @pl.loop(1, chips)
            def _(d):
                gather_chip(i, d).wait_recv()
            gather_core(i).start()
        if i >= 1:
            a = i - 1
            gather_core(a).wait_recv()
            for p, (pz, px, pc) in enumerate(places):
                piece = xbuf[pz * SIDE + px, pc, :, a * gc:(a + 1) * gc]
                x32[p * rows:(p + 1) * rows, :] = piece.astype(jnp.float32)
            for b in range(per):
                xb[a * per + b] = x32[:, b * kc:(b + 1) * kc].astype(jnp.bfloat16)
            lax.fori_loop(a * per, (a + 1) * per, multiply, 0)
    for j in range(SLOTS + EARLY_DOWN, DOWN_STEPS):
        down_copy(j).start()

    block = 256 if hid % 256 == 0 else 128
    first = hid // block // 2 * block
    spans = ((0, first), (first, hid - first))

    def exchange(src, dst, send_sem, recv_sem, b):
        cols = pl.ds(*spans[b])

        def step(d):
            target = lax.rem(me + d, n)
            return remote(src.at[target, :, cols], dst.at[me, :, cols],
                          send_sem.at[b, d - 1], recv_sem.at[b, d - 1], target)
        return step

    def begin(step):
        @pl.loop(1, n)
        def _(d):
            step(d).start()

    def end(step):
        @pl.loop(1, n)
        def _(d):
            step(d).wait()

    hbuf[...] = (jax.nn.silu(acc_g[...]) * acc_u[...]).astype(jnp.bfloat16)
    local_copy.wait()
    for b, (start, size) in enumerate(spans):
        cols = slice(start, start + size)
        acc_g[:, cols] = jnp.dot(hbuf[...], lbuf[:, cols], preferred_element_type=jnp.float32)
        for p, place in enumerate(places):
            sbuf[index(*place), :, cols] = acc_g[p * rows:(p + 1) * rows, cols].astype(jnp.bfloat16)
        begin(exchange(sbuf, rbuf, m1s, m1r, b))

    for a in range(GATHER_STEPS):
        @pl.loop(1, chips)
        def _(d):
            gather_chip(a, d).wait_send()
        gather_core(a).wait_send()

    line = lax.broadcasted_iota(jnp.int32, (rows, block), 0)
    scales = jnp.zeros((rows, block), jnp.float32)
    for r in range(rows):
        scales = jnp.where(line == r, scale[me * rows + r], scales)
    inverse = 1.0 / (1.5 * scales)
    norm = 1.0 / (float(n) ** 0.5)

    for b, (start, size) in enumerate(spans):
        rbuf[me, :, pl.ds(start, size)] = sbuf[me, :, pl.ds(start, size)]
        end(exchange(sbuf, rbuf, m1s, m1r, b))

        @pl.loop(0, size // block)
        def _(q):
            cols = pl.ds(pl.multiple_of(start + q * block, block), block)
            parts = [rbuf[s, :, cols].astype(jnp.float32) for s in range(n)]
            for level in range(n.bit_length() - 1):
                bit = 1 << level
                parts = [parts[t ^ bit] - parts[t] if t & bit else parts[t] + parts[t ^ bit] for t in range(n)]
            for t in range(n):
                c2[t, :, cols] = (1.5 * jnp.tanh((parts[t] * norm) * inverse)).astype(jnp.bfloat16)
        begin(exchange(c2, cbuf, m2s, m2r, b))

    def arrive(b):
        start, size = spans[b]
        cols = slice(start, start + size)
        cbuf[me, :, cols] = c2[me, :, cols]
        end(exchange(c2, cbuf, m2s, m2r, b))
        for p, place in enumerate(places):
            c32[p * rows:(p + 1) * rows, cols] = cbuf[index(*place), :, cols].astype(jnp.float32)
        cb[:, cols] = c32[:, cols].astype(jnp.bfloat16)

    arrive(0)
    for j in range(DOWN_STEPS):
        down_copy(j).wait()
        pacc[j] = jnp.dot(cb[:, :first], dbuf[j, :first, :], preferred_element_type=jnp.float32)
    arrive(1)

    half = n * rows // CORES
    quarter = half // SIDE

    def scatter_c(j):
        return remote(send1.at[j], rec1.at[j], r1s.at[j], r1r.at[j], index(z, x, 1 - c))

    def scatter_x(j):
        return remote(send2.at[j], rec2.at[j], r2s.at[j], r2r.at[j], index(z, 1 - x, c))

    def scatter_z(j, d):
        pz = lax.rem(z + d, zs)
        return remote(zsend.at[j, pz], zrec.at[j, d - 1], r3s.at[j, d - 1], r3r.at[j, d - 1], index(pz, x, c))

    for i in range(DOWN_STEPS + LAGS[2]):
        if i < DOWN_STEPS:
            j = i
            part = pacc[j] + jnp.dot(cb[:, first:], dbuf[j, first:, :], preferred_element_type=jnp.float32)
            keep1[j] = jnp.where(c == 1, part[half:], part[:half])
            send1[j] = jnp.where(c == 1, part[:half], part[half:]).astype(jnp.bfloat16)
            scatter_c(j).start()
        j = i - LAGS[0]
        if 0 <= j < DOWN_STEPS:
            scatter_c(j).wait()
            part = keep1[j] + rec1[j].astype(jnp.float32)
            keep2[j] = jnp.where(x == 1, part[quarter:], part[:quarter])
            send2[j] = jnp.where(x == 1, part[:quarter], part[quarter:]).astype(jnp.bfloat16)
            scatter_x(j).start()
        j = i - LAGS[1]
        if 0 <= j < DOWN_STEPS:
            scatter_x(j).wait()
            keep2[j] = keep2[j] + rec2[j].astype(jnp.float32)
            for pz in range(zs):
                piece = keep2[j, pz * rows:(pz + 1) * rows, :]
                zkeep[j, pz] = piece
                zsend[j, pz] = piece.astype(jnp.bfloat16)
            for d in range(1, zs):
                scatter_z(j, d).start()
        j = i - LAGS[2]
        if 0 <= j < DOWN_STEPS:
            total = zkeep[j, z]
            for d in range(1, zs):
                scatter_z(j, d).wait()
                total = total + zrec[j, d - 1].astype(jnp.float32)
            out[:, j * nc:(j + 1) * nc] = total.astype(jnp.bfloat16)


def kernel_body(tokens, gate_weight, up_weight, local_factor, row_scale, down_weight):
    n = lax.axis_size("tensor")
    rows, width = tokens.shape
    hid = gate_weight.shape[1]
    zs = n // (SIDE * CORES)
    kc = width // K_STEPS
    gc = width // GATHER_STEPS
    nc = width // DOWN_STEPS
    half = n * rows // CORES
    quarter = half // SIDE
    bf16, f32 = jnp.bfloat16, jnp.float32
    dma = pltpu.SemaphoreType.DMA
    vmem = pl.BlockSpec(memory_space=pltpu.VMEM)
    hbm = pl.BlockSpec(memory_space=pl.ANY)
    return pl.pallas_call(
        functools.partial(kernel, n),
        out_shape=jax.ShapeDtypeStruct((rows, width), bf16),
        in_specs=[vmem, hbm, hbm, hbm, pl.BlockSpec(memory_space=pltpu.SMEM), hbm],
        out_specs=vmem,
        scratch_shapes=[
            pltpu.VMEM((SLOTS, kc, hid), bf16),
            pltpu.VMEM((SLOTS, kc, hid), bf16),
            pltpu.VMEM((hid, hid), bf16),
            pltpu.VMEM((DOWN_STEPS, hid, nc), bf16),
            pltpu.VMEM((n // CORES, CORES, rows, width), bf16),
            pltpu.VMEM((n * rows, gc), f32),
            pltpu.VMEM((K_STEPS, n * rows, kc), bf16),
            pltpu.VMEM((n * rows, hid), f32),
            pltpu.VMEM((n * rows, hid), f32),
            pltpu.VMEM((n * rows, hid), bf16),
            pltpu.VMEM((n, rows, hid), bf16),
            pltpu.VMEM((n, rows, hid), bf16),
            pltpu.VMEM((n, rows, hid), bf16),
            pltpu.VMEM((n, rows, hid), bf16),
            pltpu.VMEM((n * rows, hid), f32),
            pltpu.VMEM((n * rows, hid), bf16),
            pltpu.VMEM((DOWN_STEPS, n * rows, nc), f32),
            pltpu.VMEM((DOWN_STEPS, half, nc), f32),
            pltpu.VMEM((DOWN_STEPS, half, nc), bf16),
            pltpu.VMEM((DOWN_STEPS, half, nc), bf16),
            pltpu.VMEM((DOWN_STEPS, quarter, nc), f32),
            pltpu.VMEM((DOWN_STEPS, quarter, nc), bf16),
            pltpu.VMEM((DOWN_STEPS, quarter, nc), bf16),
            pltpu.VMEM((DOWN_STEPS, zs, rows, nc), f32),
            pltpu.VMEM((DOWN_STEPS, zs, rows, nc), bf16),
            pltpu.VMEM((DOWN_STEPS, zs - 1, rows, nc), bf16),
            dma((SLOTS,)), dma((SLOTS,)), dma, dma((DOWN_STEPS,)), dma,
            dma((GATHER_STEPS, n // CORES - 1)), dma((GATHER_STEPS, n // CORES - 1)),
            dma((GATHER_STEPS,)), dma((GATHER_STEPS,)),
            dma((2, n - 1)), dma((2, n - 1)), dma((2, n - 1)), dma((2, n - 1)),
            dma((DOWN_STEPS,)), dma((DOWN_STEPS,)),
            dma((DOWN_STEPS,)), dma((DOWN_STEPS,)),
            dma((DOWN_STEPS, zs - 1)), dma((DOWN_STEPS, zs - 1)),
        ],
        compiler_params=pltpu.CompilerParams(
            collective_id=0, has_side_effects=True, vmem_limit_bytes=67043328),
    )(tokens, gate_weight, up_weight, local_factor, row_scale, down_weight)


def body(tokens, gate_weight, up_weight, local_factor, row_scale, down_weight):
    n = lax.axis_size("tensor")
    rows, width = tokens.shape
    hid = gate_weight.shape[1]
    fits = (n == 1 << (n.bit_length() - 1) and n % (SIDE * CORES * 2) == 0 and hid % 256 == 0 and hid > 256
            and width % (128 * K_STEPS) == 0 and n * rows <= 32)
    chosen = kernel_body if fits else plain_body
    return chosen(tokens, gate_weight, up_weight, local_factor, row_scale, down_weight)


def solution(mesh):
    in_specs = (
        P(("groups", "tensor"), None),
        P(None, "tensor"),
        P(None, "tensor"),
        P(),
        P("groups"),
        P("tensor", None),
    )
    out_specs = P(("groups", "tensor"), None)
    return jax.shard_map(body, mesh=mesh, in_specs=in_specs, out_specs=out_specs, check_vma=False)
```
